32 devices in a mesh: groups: 2 (over x), blk: 16 (over z, y, core).
Axes of the slice: x: 2, y: 2, z: 4, core: 2. Of those that a mesh axis runs over, the one named last changes fastest.
Arguments:
- frames: bfloat16 [256, 16384], P(('groups', 'blk')), parts along dimension 0
- basis: bfloat16 [256, 64], P(('groups', 'blk')), parts along dimension 0, may hold values from -6 to 6
- density: bfloat16 [256], P(('groups', 'blk')), parts along dimension 0, may hold values from 0.25 to 4
Outputs:
- residual_block: bfloat16 [256, 64], P(('groups', 'blk')), parts along dimension 0
- coefficients: float32 [128, 64], P('groups'), parts along dimension 0
The draws below stay inside these ranges and needn't reach their ends.
There are 2 independent parts, one for each index of `groups`. The reference program is written for one: setup_inputs(seed, part) draws one part's arguments, and reference() takes and returns one part's arrays. A program takes and returns all parts, laid end to end along the dimension named above; each array names one. Nothing has to cross between parts.
All inputs are finite; a program needn't handle non-finite values.
Results may differ from the reference program's by a relative error of at most 0.0045.
Values may be sent and summed in bfloat16 or wider, within the bound.
No kernel may reach another device: no remote copies, remote signals or barrier semaphores. Data moves between devices by JAX's collectives and lax.ppermute only.
A program may use at most 64 MiB of HBM per device.

```python
import math
import jax
import jax.numpy as jnp
from jax import lax

F = 16384
BASIS = 64
ROWS = 8
FRAMES = 128
N_BLK = 16


def draw_frames(key, part):
    key_time = jax.random.fold_in(key, 21)
    key_freq = jax.random.fold_in(key, 22)
    key_phase = jax.random.fold_in(key, 23)
    key_jitter = jax.random.fold_in(key, 24)
    span = FRAMES / 16.0
    amplitude = math.sqrt(6.0)
    times = jax.random.uniform(key_time, (FRAMES, 1), jnp.float32, 0.0, span)
    spread = jax.random.uniform(key_freq, (1, F), jnp.float32, -0.49, 0.49)
    omega = jnp.tan(math.pi * spread)
    phase = jax.random.uniform(key_phase, (1, F), jnp.float32, -math.pi, math.pi)
    jitter = 0.25 * jax.random.normal(key_jitter, (FRAMES, F), jnp.float32)
    features = amplitude * jnp.cos(times * omega + phase) + jitter
    return features.astype(jnp.bfloat16)


def shard_levels(stream_key, dims, pieces, low, top_value):
    factor_of, own = 1.0, jax.random.fold_in(stream_key, 6)
    for dim, parts in pieces:
        steps = jnp.exp(jax.random.uniform(jax.random.fold_in(own, dim), (parts,), jnp.float32, low / len(pieces), top_value / len(pieces)))
        factor_of = factor_of * jnp.repeat(steps, dims[dim] // parts).reshape([-1 if axis == dim else 1 for axis in range(len(dims))])
    return factor_of


def bell_draw(own_key, shape, scale, limit, cuts=(), held_as=jnp.bfloat16):
    entries = scale * jax.random.normal(own_key, shape, jnp.float32)
    if cuts:
        entries = entries * shard_levels(own_key, shape, cuts, -0.22, 0.18)
    return jnp.clip(entries, -limit, limit).astype(held_as)


def setup_inputs(seed: int = 0, part: int = 0) -> dict:
    arg_keys = jax.random.split(jax.random.key(seed), 4)
    part_splits = jax.random.split(jax.random.fold_in(arg_keys[3], part), 4)
    return {
        "frames": draw_frames(jax.random.fold_in(jax.random.fold_in(arg_keys[3], part), 71), part),
        "basis": bell_draw(part_splits[1], (FRAMES, BASIS), 1.0, 6.0, ((0, 16),)),
        "density": jnp.clip(jnp.exp(math.log(4.0) - 2.7725887 * jax.random.uniform(part_splits[2], (FRAMES,), jnp.float32) ** shard_levels(part_splits[2], (FRAMES,), ((0, 16),), -0.2, 0.2)), 0.25, 4.0).astype(jnp.bfloat16),
    }


def reference(frames, basis, density):
    norms = jnp.sum(jnp.square(frames.astype(jnp.float32)), axis=1)
    density_f = density.astype(jnp.float32)

    def one_block(block_index):
        block_rows = lax.dynamic_slice_in_dim(frames, block_index * ROWS, ROWS, 0)
        block_norms = lax.dynamic_slice_in_dim(norms, block_index * ROWS, ROWS, 0)
        inner_products = lax.dot_general(block_rows, frames, (((1,), (1,)), ((), ())), preferred_element_type=jnp.float32)
        squared_dist = block_norms[:, None] + norms[None, :] - 2.0 * inner_products
        weight = (jnp.exp(-squared_dist / F) * density_f[None, :]).astype(jnp.bfloat16)
        numer = jnp.dot(weight, basis, preferred_element_type=jnp.float32)
        totals = jnp.sum(weight.astype(jnp.float32), axis=1)
        return numer / totals[:, None]

    applied = lax.map(one_block, jnp.arange(N_BLK, dtype=jnp.int32)).reshape(FRAMES, BASIS)
    basis_f = basis.astype(jnp.float32)
    coefficients = lax.dot_general(basis_f, applied, (((0,), (0,)), ((), ())), precision=lax.Precision.HIGHEST, preferred_element_type=jnp.float32)
    projection = jnp.dot(basis_f, coefficients, precision=lax.Precision.HIGHEST, preferred_element_type=jnp.float32)
    residual_block = (applied - projection / FRAMES).astype(jnp.bfloat16)
    return residual_block, coefficients
```

```python
import functools

import jax
import jax.numpy as jnp
from jax import lax
from jax.experimental import pallas as pl
from jax.experimental.pallas import tpu as pltpu
from jax.sharding import PartitionSpec as P


def partial_kernel(count, features_ref, basis_ref, density_ref, message_ref):
    features = features_ref[...]
    total = features.shape[0]
    half = total // 2
    rows, width = basis_ref.shape
    inner = lax.dot_general(
        features, features, (((1,), (1,)), ((), ())), preferred_element_type=jnp.float32
    )
    row = lax.broadcasted_iota(jnp.int32, (total, total), 0)
    lane = lax.broadcasted_iota(jnp.int32, (total, total), 1)
    diagonal = jnp.where(row == lane, inner, 0.0)
    dist = (
        jnp.sum(diagonal, axis=1, keepdims=True)
        + jnp.sum(diagonal, axis=0, keepdims=True)
        - 2.0 * inner
    )
    top, bottom = dist[:half], pltpu.roll(dist[half:], half, 1)
    own_row, own_lane = row[:half], lane[:half]
    packed = jnp.where((own_lane < half) & (own_row >= own_lane), bottom, top)

    me = lax.axis_index("blk")
    vectors = jnp.concatenate(
        [
            basis_ref[...].astype(jnp.float32),
            jnp.ones((rows, 1), jnp.float32),
            jnp.zeros((rows, total - width - 1), jnp.float32),
        ],
        axis=1,
    )
    density = density_ref[...].astype(jnp.float32).reshape(1, rows)
    spread = jnp.concatenate([density, jnp.zeros((1, total - rows), jnp.float32)], axis=1)
    spread = pltpu.roll(jnp.broadcast_to(spread, (rows, total)), me * rows, 1)
    message = jnp.concatenate([packed, vectors, spread], axis=0).astype(jnp.bfloat16)
    for peer in range(count):
        message_ref[peer] = message


def finish_kernel(count, feature_count, rows, width, received_ref, residual_ref, coef_ref, applied_ref):
    total = count * rows
    half = total // 2
    packed = received_ref[0, :half].astype(jnp.float32)
    density = received_ref[0, half:].astype(jnp.float32)[rows : rows + 1]
    for peer in range(1, count):
        packed += received_ref[peer, :half].astype(jnp.float32)
        density += received_ref[peer, half:].astype(jnp.float32)[rows : rows + 1]
    row = lax.broadcasted_iota(jnp.int32, (half, total), 0)
    lane = lax.broadcasted_iota(jnp.int32, (half, total), 1)
    top = jnp.where((lane >= half) | (row < lane), packed, 0.0)
    bottom = pltpu.roll(jnp.where((lane < half) & (row > lane), packed, 0.0), half, 1)
    one_side = jnp.concatenate([top, bottom], axis=0)
    dist = one_side + one_side.T
    weight = (jnp.exp(-dist / feature_count) * density).astype(jnp.bfloat16)
    vectors = jnp.concatenate(
        [received_ref[peer, half:].astype(jnp.float32)[:rows, :128] for peer in range(count)], axis=0
    )
    numer = jnp.dot(weight, vectors.astype(jnp.bfloat16), preferred_element_type=jnp.float32)
    applied = numer[:, :width] / numer[:, width : width + 1]
    applied_ref[...] = applied
    coef = lax.dot_general(
        vectors[:, :width],
        applied,
        (((0,), (0,)), ((), ())),
        precision=lax.Precision.HIGHEST,
        preferred_element_type=jnp.float32,
    )
    coef_ref[...] = coef
    me = lax.axis_index("blk")
    own = received_ref[me, half:].astype(jnp.float32)[:rows, :width]
    projection = jnp.dot(
        own, coef, precision=lax.Precision.HIGHEST, preferred_element_type=jnp.float32
    )
    own_applied = applied_ref[pl.ds(pl.multiple_of(me * rows, rows), rows), :]
    residual_ref[...] = (own_applied - projection / total).astype(jnp.bfloat16)


def shards(frames, basis, density):
    count = lax.axis_size("blk")
    rows, feature_count = frames.shape
    width = basis.shape[1]
    total = rows * count
    whole = pl.BlockSpec(memory_space=pltpu.VMEM)
    params = pltpu.CompilerParams(vmem_limit_bytes=48 << 20)
    features = lax.all_to_all(frames, "blk", split_axis=1, concat_axis=0, tiled=True)
    message = pl.pallas_call(
        functools.partial(partial_kernel, count),
        out_shape=jax.ShapeDtypeStruct((count, total // 2 + 2 * rows, total), jnp.bfloat16),
        in_specs=[whole] * 3,
        out_specs=whole,
        compiler_params=params,
    )(features, basis, density)
    received = lax.all_to_all(message, "blk", split_axis=0, concat_axis=0, tiled=True)
    return pl.pallas_call(
        functools.partial(finish_kernel, count, feature_count, rows, width),
        out_shape=(
            jax.ShapeDtypeStruct((rows, width), jnp.bfloat16),
            jax.ShapeDtypeStruct((width, width), jnp.float32),
        ),
        in_specs=[whole],
        out_specs=(whole, whole),
        scratch_shapes=[pltpu.VMEM((total, width), jnp.float32)],
        compiler_params=params,
    )(received)


def solution(mesh):
    placed = (P(("groups", "blk"), None), P(("groups", "blk"), None), P(("groups", "blk")))
    return jax.shard_map(
        shards,
        mesh=mesh,
        in_specs=placed,
        out_specs=(P(("groups", "blk"), None), P("groups", None)),
        check_vma=False,
    )
```

```python
import functools

import jax
import jax.numpy as jnp
from jax import lax
from jax.experimental import pallas as pl
from jax.experimental.pallas import tpu as pltpu
from jax.sharding import PartitionSpec as P


def partial_kernel(features_ref, basis_ref, density_ref, message_ref):
    features = features_ref[...]
    total = features.shape[0]
    half = total // 2
    rows, width = basis_ref.shape
    inner = lax.dot_general(
        features, features, (((1,), (1,)), ((), ())), preferred_element_type=jnp.float32
    )
    row = lax.broadcasted_iota(jnp.int32, (total, total), 0)
    lane = lax.broadcasted_iota(jnp.int32, (total, total), 1)
    diagonal = jnp.where(row == lane, inner, 0.0)
    dist = (
        jnp.sum(diagonal, axis=1, keepdims=True)
        + jnp.sum(diagonal, axis=0, keepdims=True)
        - 2.0 * inner
    )
    top, bottom = dist[:half], pltpu.roll(dist[half:], half, 1)
    own_row, own_lane = row[:half], lane[:half]
    packed = jnp.where((own_lane < half) & (own_row >= own_lane), bottom, top)

    me = lax.axis_index("blk")
    density = density_ref[...].astype(jnp.float32).reshape(1, rows)
    density = jnp.concatenate([density, jnp.zeros((1, total - rows), jnp.float32)], axis=1)
    density = pltpu.roll(density, lax.rem(me * rows, half), 1)
    packed = jnp.where(own_row == own_lane, density, packed)
    vectors = jnp.concatenate(
        [basis_ref[...].astype(jnp.float32), jnp.zeros((rows, total - width), jnp.float32)], axis=1
    )
    message_ref[:half] = packed
    message_ref[half:] = pltpu.roll(vectors, lax.rem(me, 2) * width, 1)


def finish_kernel(feature_count, width, received_ref, residual_ref, coef_ref, applied_ref, vectors_ref):
    pairs, height, total = received_ref.shape
    half = total // 2
    rows = height - half
    first = sum(received_ref[pair, :half].astype(jnp.float32) for pair in range(pairs // 2))
    second = sum(received_ref[pair, :half].astype(jnp.float32) for pair in range(pairs // 2, pairs))
    packed = first + second
    row = lax.broadcasted_iota(jnp.int32, (half, total), 0)
    lane = lax.broadcasted_iota(jnp.int32, (half, total), 1)
    slots = jnp.where(row == lane, first, 0.0) + pltpu.roll(
        jnp.where(row == lane, second, 0.0), half, 1
    )
    density = jnp.sum(slots, axis=0, keepdims=True)
    top = jnp.where((lane >= half) | (row < lane), packed, 0.0)
    bottom = pltpu.roll(jnp.where((lane < half) & (row > lane), packed, 0.0), half, 1)
    one_side = jnp.concatenate([top, bottom], axis=0)
    dist = one_side + one_side.T
    weight = (jnp.exp(-dist / feature_count) * density).astype(jnp.bfloat16)
    for pair in range(pairs):
        both = received_ref[pair, half:].astype(jnp.float32)
        vectors_ref[2 * pair * rows : (2 * pair + 1) * rows] = both[:, :width]
        vectors_ref[(2 * pair + 1) * rows : (2 * pair + 2) * rows] = both[:, width : 2 * width]
    vectors = vectors_ref[...]
    extended = jnp.concatenate(
        [vectors, jnp.ones((total, 1), jnp.float32), jnp.zeros((total, width - 1), jnp.float32)], axis=1
    )
    numer = jnp.dot(weight, extended.astype(jnp.bfloat16), preferred_element_type=jnp.float32)
    applied = numer[:, :width] / numer[:, width : width + 1]
    applied_ref[...] = applied
    coef = lax.dot_general(
        vectors,
        applied,
        (((0,), (0,)), ((), ())),
        precision=lax.Precision.HIGHEST,
        preferred_element_type=jnp.float32,
    )
    coef_ref[...] = coef
    me = lax.axis_index("blk")
    own_rows = pl.ds(pl.multiple_of(me * rows, rows), rows)
    projection = jnp.dot(
        vectors_ref[own_rows, :],
        coef,
        precision=lax.Precision.HIGHEST,
        preferred_element_type=jnp.float32,
    )
    residual_ref[...] = (applied_ref[own_rows, :] - projection / total).astype(jnp.bfloat16)


def shards(frames, basis, density):
    count = lax.axis_size("blk")
    rows, feature_count = frames.shape
    width = basis.shape[1]
    total = rows * count
    whole = pl.BlockSpec(memory_space=pltpu.VMEM)
    params = pltpu.CompilerParams(vmem_limit_bytes=48 << 20)
    features = lax.all_to_all(frames, "blk", split_axis=1, concat_axis=0, tiled=True)
    partial = pl.pallas_call(
        partial_kernel,
        out_shape=jax.ShapeDtypeStruct((total // 2 + rows, total), jnp.float32),
        in_specs=[whole] * 3,
        out_specs=whole,
        compiler_params=params,
    )(features, basis, density)
    partial += lax.ppermute(partial, "blk", [(i, i ^ 1) for i in range(count)])
    pairs = count // 2
    message = jnp.broadcast_to(partial.astype(jnp.bfloat16), (pairs, *partial.shape))
    received = lax.all_to_all(
        message,
        "blk",
        split_axis=0,
        concat_axis=0,
        tiled=True,
        axis_index_groups=[list(range(core, count, 2)) for core in range(2)],
    )
    return pl.pallas_call(
        functools.partial(finish_kernel, feature_count, width),
        out_shape=(
            jax.ShapeDtypeStruct((rows, width), jnp.bfloat16),
            jax.ShapeDtypeStruct((width, width), jnp.float32),
        ),
        in_specs=[whole],
        out_specs=(whole, whole),
        scratch_shapes=[pltpu.VMEM((total, width), jnp.float32)] * 2,
        compiler_params=params,
    )(received)


def solution(mesh):
    placed = (P(("groups", "blk"), None), P(("groups", "blk"), None), P(("groups", "blk")))
    return jax.shard_map(
        shards,
        mesh=mesh,
        in_specs=placed,
        out_specs=(P(("groups", "blk"), None), P("groups", None)),
        check_vma=False,
    )
```

```python
import functools

import jax
import jax.numpy as jnp
from jax import lax
from jax.experimental import pallas as pl
from jax.experimental.pallas import tpu as pltpu
from jax.sharding import PartitionSpec as P

PLANE = 4


def partial_kernel(features_ref, basis_hbm, density_hbm, message_ref, basis_ref, density_ref, sems):
    copies = [
        pltpu.make_async_copy(basis_hbm, basis_ref, sems.at[0]),
        pltpu.make_async_copy(density_hbm, density_ref, sems.at[1]),
    ]
    for copy in copies:
        copy.start()
    features = features_ref[...]
    total = features.shape[0]
    half = total // 2
    rows, width = basis_ref.shape
    inner = lax.dot_general(
        features, features, (((1,), (1,)), ((), ())), preferred_element_type=jnp.float32
    )
    row = lax.broadcasted_iota(jnp.int32, (total, total), 0)
    lane = lax.broadcasted_iota(jnp.int32, (total, total), 1)
    diagonal = jnp.where(row == lane, inner, 0.0)
    dist = (
        jnp.sum(diagonal, axis=1, keepdims=True)
        + jnp.sum(diagonal, axis=0, keepdims=True)
        - 2.0 * inner
    )
    top, bottom = dist[:half], pltpu.roll(dist[half:], half, 1)
    own_row, own_lane = row[:half], lane[:half]
    packed = jnp.where((own_lane < half) & (own_row >= own_lane), bottom, top)

    for copy in copies:
        copy.wait()
    me = lax.axis_index("blk")
    density = density_ref[...].astype(jnp.float32).reshape(1, rows)
    density = jnp.concatenate([density, jnp.zeros((1, total - rows), jnp.float32)], axis=1)
    density = pltpu.roll(density, lax.rem(me * rows, half), 1)
    message_ref[:half] = jnp.where(own_row == own_lane, density, packed)
    place = lax.rem(me, PLANE)
    vectors = jnp.concatenate(
        [basis_ref[...].astype(jnp.float32), jnp.zeros((rows, total - width), jnp.float32)], axis=1
    )
    vectors = pltpu.roll(vectors, lax.rem(place, 2) * width, 1)
    message_ref[half : half + rows] = jnp.where(place < 2, vectors, 0.0)
    message_ref[half + rows :] = jnp.where(place < 2, 0.0, vectors)


def finish_kernel(feature_count, width, rows, *refs):
    planes = len(refs) - 4
    message_refs = refs[:planes]
    residual_ref, coef_ref, applied_ref, vectors_ref = refs[planes:]
    total = message_refs[0].shape[1]
    half = total // 2
    me = lax.axis_index("blk")
    plane = lax.div(me, PLANE)
    near = sum(ref[:half].astype(jnp.float32) for ref in message_refs[: planes // 2])
    far = sum(ref[:half].astype(jnp.float32) for ref in message_refs[planes // 2 :])
    packed = near + far
    row = lax.broadcasted_iota(jnp.int32, (half, total), 0)
    lane = lax.broadcasted_iota(jnp.int32, (half, total), 1)
    slots = [
        jnp.sum(jnp.where(row == lane, part, 0.0), axis=0, keepdims=True) for part in (near, far)
    ]
    upper = lax.div(plane, planes // 2)
    density = pltpu.roll(slots[0], upper * half, 1) + pltpu.roll(slots[1], (1 - upper) * half, 1)
    top = jnp.where((lane >= half) | (row < lane), packed, 0.0)
    bottom = pltpu.roll(jnp.where((lane < half) & (row > lane), packed, 0.0), half, 1)
    one_side = jnp.concatenate([top, bottom], axis=0)
    dist = one_side + one_side.T
    weight = (jnp.exp(-dist / feature_count) * density).astype(jnp.bfloat16)
    for offset, ref in enumerate(message_refs):
        tail = ref[half:].astype(jnp.float32)
        base = (plane ^ offset) * PLANE * rows
        for place in range(PLANE):
            block = tail[place // 2 * rows :][:rows, place % 2 * width :][:, :width]
            vectors_ref[pl.ds(pl.multiple_of(base + place * rows, rows), rows), :] = block
    vectors = vectors_ref[...]
    extended = jnp.concatenate(
        [vectors, jnp.ones((total, 1), jnp.float32), jnp.zeros((total, width - 1), jnp.float32)], axis=1
    )
    numer = jnp.dot(weight, extended.astype(jnp.bfloat16), preferred_element_type=jnp.float32)
    applied = numer[:, :width] / numer[:, width : width + 1]
    applied_ref[...] = applied
    coef = lax.dot_general(
        vectors,
        applied,
        (((0,), (0,)), ((), ())),
        precision=lax.Precision.HIGHEST,
        preferred_element_type=jnp.float32,
    )
    coef_ref[...] = coef
    own_rows = pl.ds(pl.multiple_of(me * rows, rows), rows)
    projection = jnp.dot(
        vectors_ref[own_rows, :],
        coef,
        precision=lax.Precision.HIGHEST,
        preferred_element_type=jnp.float32,
    )
    residual_ref[...] = (applied_ref[own_rows, :] - projection / total).astype(jnp.bfloat16)


def from_peer(value, count, offset):
    return lax.ppermute(value, "blk", [(i, i ^ offset) for i in range(count)])


def shards(frames, basis, density):
    count = lax.axis_size("blk")
    rows, feature_count = frames.shape
    width = basis.shape[1]
    total = rows * count
    whole = pl.BlockSpec(memory_space=pltpu.VMEM)
    params = pltpu.CompilerParams(vmem_limit_bytes=48 << 20)
    features = lax.all_to_all(frames, "blk", split_axis=1, concat_axis=0, tiled=True)
    partial = pl.pallas_call(
        partial_kernel,
        out_shape=jax.ShapeDtypeStruct((total // 2 + 2 * rows, total), jnp.float32),
        in_specs=[whole] + [pl.BlockSpec(memory_space=pltpu.HBM)] * 2,
        out_specs=whole,
        scratch_shapes=[
            pltpu.VMEM(basis.shape, basis.dtype),
            pltpu.VMEM(density.shape, density.dtype),
            pltpu.SemaphoreType.DMA((2,)),
        ],
        compiler_params=params,
    )(
        features,
        pltpu.with_memory_space_constraint(basis, pltpu.HBM),
        pltpu.with_memory_space_constraint(density, pltpu.HBM),
    )
    peers = [from_peer(partial, count, offset) for offset in range(1, PLANE)]
    message = sum(peers, partial).astype(jnp.bfloat16)
    messages = [message] + [
        from_peer(message, count, offset) for offset in range(PLANE, count, PLANE)
    ]
    return pl.pallas_call(
        functools.partial(finish_kernel, feature_count, width, rows),
        out_shape=(
            jax.ShapeDtypeStruct((rows, width), jnp.bfloat16),
            jax.ShapeDtypeStruct((width, width), jnp.float32),
        ),
        in_specs=[whole] * len(messages),
        out_specs=(whole, whole),
        scratch_shapes=[pltpu.VMEM((total, width), jnp.float32)] * 2,
        compiler_params=params,
    )(*messages)


def solution(mesh):
    placed = (P(("groups", "blk"), None), P(("groups", "blk"), None), P(("groups", "blk")))
    return jax.shard_map(
        shards,
        mesh=mesh,
        in_specs=placed,
        out_specs=(P(("groups", "blk"), None), P("groups", None)),
        check_vma=False,
    )
```

```python
import functools

import jax
import jax.numpy as jnp
from jax import lax
from jax.experimental import pallas as pl
from jax.experimental.pallas import tpu as pltpu
from jax.sharding import PartitionSpec as P

CORES = 2


def partial_kernel(features_ref, basis_hbm, density_hbm, message_ref, basis_ref, density_ref, sems):
    copies = [
        pltpu.make_async_copy(basis_hbm, basis_ref, sems.at[0]),
        pltpu.make_async_copy(density_hbm, density_ref, sems.at[1]),
    ]
    for copy in copies:
        copy.start()
    features = features_ref[...]
    total = features.shape[0]
    half = total // 2
    rows, width = basis_ref.shape
    inner = lax.dot_general(
        features, features, (((1,), (1,)), ((), ())), preferred_element_type=jnp.float32
    )
    row = lax.broadcasted_iota(jnp.int32, (total, total), 0)
    lane = lax.broadcasted_iota(jnp.int32, (total, total), 1)
    diagonal = jnp.where(row == lane, inner, 0.0)
    dist = (
        jnp.sum(diagonal, axis=1, keepdims=True)
        + jnp.sum(diagonal, axis=0, keepdims=True)
        - 2.0 * inner
    )
    top, bottom = dist[:half], pltpu.roll(dist[half:], half, 1)
    own_row, own_lane = row[:half], lane[:half]
    packed = jnp.where((own_lane < half) & (own_row >= own_lane), bottom, top)

    for copy in copies:
        copy.wait()
    me = lax.axis_index("blk")
    density = density_ref[...].astype(jnp.float32).reshape(1, rows)
    density = jnp.concatenate([density, jnp.zeros((1, total - rows), jnp.float32)], axis=1)
    density = pltpu.roll(density, lax.rem(me * rows, half), 1)
    message_ref[:half] = jnp.where(own_row == own_lane, density, packed)
    vectors = jnp.concatenate(
        [basis_ref[...].astype(jnp.float32), jnp.zeros((rows, total - width), jnp.float32)], axis=1
    )
    message_ref[half:] = pltpu.roll(vectors, lax.rem(me, CORES) * width, 1)


def routes(pairs):
    evens = [offset for offset in range(pairs) if offset.bit_count() % 2 == 0]
    return [(offset, offset ^ (1 if offset < pairs // 2 else 2)) for offset in evens]


def finish_kernel(feature_count, width, rows, *refs):
    residual_ref, coef_ref, applied_ref, vectors_ref = refs[-4:]
    own_ref, *message_refs = refs[:-4]
    half = own_ref.shape[1] // 2
    total = 2 * half
    pairs = total // (CORES * rows)
    me = lax.axis_index("blk")
    core, pair = lax.rem(me, CORES), lax.div(me, CORES)
    steps = routes(pairs)
    steps = steps + [(two, one) for one, two in steps]
    near = own_ref[:half].astype(jnp.float32)
    far = jnp.zeros_like(near)
    for step, ref in zip(steps, message_refs):
        if max(step) < pairs // 2:
            near += ref[:half].astype(jnp.float32)
        else:
            far += ref[:half].astype(jnp.float32)
    packed = near + far
    row = lax.broadcasted_iota(jnp.int32, (half, total), 0)
    lane = lax.broadcasted_iota(jnp.int32, (half, total), 1)
    slots = [
        jnp.sum(jnp.where(row == lane, part, 0.0), axis=0, keepdims=True) for part in (near, far)
    ]
    upper = lax.div(pair, pairs // 2)
    density = pltpu.roll(slots[0], upper * half, 1) + pltpu.roll(slots[1], (1 - upper) * half, 1)
    top = jnp.where((lane >= half) | (row < lane), packed, 0.0)
    bottom = pltpu.roll(jnp.where((lane < half) & (row > lane), packed, 0.0), half, 1)
    one_side = jnp.concatenate([top, bottom], axis=0)
    dist = one_side + one_side.T
    weight = (jnp.exp(-dist / feature_count) * density).astype(jnp.bfloat16)
    for step, ref in zip(steps + [(0, 0)], message_refs + [own_ref]):
        both = ref[half:].astype(jnp.float32)
        base = (pair ^ jnp.where(core == 0, step[0], step[1])) * CORES * rows
        for place in range(CORES):
            block = both[:, place * width : (place + 1) * width]
            vectors_ref[pl.ds(pl.multiple_of(base + place * rows, rows), rows), :] = block
    vectors = vectors_ref[...]
    extended = jnp.concatenate(
        [vectors, jnp.ones((total, 1), jnp.float32), jnp.zeros((total, width - 1), jnp.float32)], axis=1
    )
    numer = jnp.dot(weight, extended.astype(jnp.bfloat16), preferred_element_type=jnp.float32)
    applied = numer[:, :width] / numer[:, width : width + 1]
    applied_ref[...] = applied
    coef = lax.dot_general(
        vectors,
        applied,
        (((0,), (0,)), ((), ())),
        precision=lax.Precision.HIGHEST,
        preferred_element_type=jnp.float32,
    )
    coef_ref[...] = coef
    own_rows = pl.ds(pl.multiple_of(me * rows, rows), rows)
    projection = jnp.dot(
        vectors_ref[own_rows, :],
        coef,
        precision=lax.Precision.HIGHEST,
        preferred_element_type=jnp.float32,
    )
    residual_ref[...] = (applied_ref[own_rows, :] - projection / total).astype(jnp.bfloat16)


def from_peer(value, count, offsets):
    links = [(i, i ^ offsets[i % CORES]) for i in range(count) if offsets[i % CORES]]
    return lax.ppermute(value, "blk", links)


def shards(frames, basis, density):
    count = lax.axis_size("blk")
    rows, feature_count = frames.shape
    width = basis.shape[1]
    total = rows * count
    whole = pl.BlockSpec(memory_space=pltpu.VMEM)
    params = pltpu.CompilerParams(vmem_limit_bytes=48 << 20)
    features = lax.all_to_all(frames, "blk", split_axis=1, concat_axis=0, tiled=True)
    partial = pl.pallas_call(
        partial_kernel,
        out_shape=jax.ShapeDtypeStruct((total // 2 + rows, total), jnp.float32),
        in_specs=[whole] + [pl.BlockSpec(memory_space=pltpu.HBM)] * 2,
        out_specs=whole,
        scratch_shapes=[
            pltpu.VMEM(basis.shape, basis.dtype),
            pltpu.VMEM(density.shape, density.dtype),
            pltpu.SemaphoreType.DMA((2,)),
        ],
        compiler_params=params,
    )(
        features,
        pltpu.with_memory_space_constraint(basis, pltpu.HBM),
        pltpu.with_memory_space_constraint(density, pltpu.HBM),
    )
    sibling = (1, 1)
    message = (partial + from_peer(partial, count, sibling)).astype(jnp.bfloat16)
    received = [
        from_peer(message, count, (CORES * first, CORES * second))
        for first, second in routes(count // CORES)
    ]
    messages = [message] + received + [from_peer(part, count, sibling) for part in received]
    return pl.pallas_call(
        functools.partial(finish_kernel, feature_count, width, rows),
        out_shape=(
            jax.ShapeDtypeStruct((rows, width), jnp.bfloat16),
            jax.ShapeDtypeStruct((width, width), jnp.float32),
        ),
        in_specs=[whole] * len(messages),
        out_specs=(whole, whole),
        scratch_shapes=[pltpu.VMEM((total, width), jnp.float32)] * 2,
        compiler_params=params,
    )(*messages)


def solution(mesh):
    placed = (P(("groups", "blk"), None), P(("groups", "blk"), None), P(("groups", "blk")))
    return jax.shard_map(
        shards,
        mesh=mesh,
        in_specs=placed,
        out_specs=(P(("groups", "blk"), None), P("groups", None)),
        check_vma=False,
    )
```

```python
import functools

import jax
import jax.numpy as jnp
from jax import lax
from jax.experimental import pallas as pl
from jax.experimental.pallas import tpu as pltpu
from jax.sharding import PartitionSpec as P

CORES = 2


def partial_kernel(features_ref, basis_hbm, density_hbm, message_ref, basis_ref, density_ref, sems):
    copies = [
        pltpu.make_async_copy(basis_hbm, basis_ref, sems.at[0]),
        pltpu.make_async_copy(density_hbm, density_ref, sems.at[1]),
    ]
    for copy in copies:
        copy.start()
    features = features_ref[...]
    total = features.shape[0]
    half = total // 2
    rows, width = basis_ref.shape
    inner = lax.dot_general(
        features, features, (((1,), (1,)), ((), ())), preferred_element_type=jnp.float32
    )
    row = lax.broadcasted_iota(jnp.int32, (total, total), 0)
    lane = lax.broadcasted_iota(jnp.int32, (total, total), 1)
    diagonal = jnp.where(row == lane, inner, 0.0)
    dist = (
        jnp.sum(diagonal, axis=1, keepdims=True)
        + jnp.sum(diagonal, axis=0, keepdims=True)
        - 2.0 * inner
    )
    top, bottom = dist[:half], pltpu.roll(dist[half:], half, 1)
    own_row, own_lane = row[:half], lane[:half]
    packed = jnp.where((own_lane < half) & (own_row >= own_lane), bottom, top)

    for copy in copies:
        copy.wait()
    me = lax.axis_index("blk")
    density = density_ref[...].astype(jnp.float32).reshape(1, rows)
    density = jnp.concatenate([density, jnp.zeros((1, total - rows), jnp.float32)], axis=1)
    density = pltpu.roll(density, lax.rem(me * rows, half), 1)
    message_ref[:half] = jnp.where(own_row == own_lane, density, packed)
    vectors = jnp.concatenate(
        [basis_ref[...].astype(jnp.float32), jnp.zeros((rows, total - width), jnp.float32)], axis=1
    )
    message_ref[half:] = pltpu.roll(vectors, lax.rem(me, CORES) * width, 1)


def routes(pairs):
    evens = [offset for offset in range(pairs) if offset.bit_count() % 2 == 0]
    return [(offset, offset ^ (1 if offset < pairs // 2 else 2)) for offset in evens]


def pieces(value):
    high = value.astype(jnp.bfloat16).astype(jnp.float32)
    middle = (value - high).astype(jnp.bfloat16).astype(jnp.float32)
    return high, middle, (value - high - middle).astype(jnp.bfloat16).astype(jnp.float32)


def finish_kernel(feature_count, width, rows, *refs):
    residual_ref, coef_ref, applied_ref, vectors_ref = refs[-4:]
    own_ref, *message_refs = refs[:-4]
    half = own_ref.shape[1] // 2
    total = 2 * half
    pairs = total // (CORES * rows)
    me = lax.axis_index("blk")
    core, pair = lax.rem(me, CORES), lax.div(me, CORES)
    steps = routes(pairs)
    steps = steps + [(two, one) for one, two in steps]
    near = own_ref[:half].astype(jnp.float32)
    far = jnp.zeros_like(near)
    for step, ref in zip(steps, message_refs):
        if max(step) < pairs // 2:
            near += ref[:half].astype(jnp.float32)
        else:
            far += ref[:half].astype(jnp.float32)
    packed = near + far
    row = lax.broadcasted_iota(jnp.int32, (half, total), 0)
    lane = lax.broadcasted_iota(jnp.int32, (half, total), 1)
    slots = [
        jnp.sum(jnp.where(row == lane, part, 0.0), axis=0, keepdims=True) for part in (near, far)
    ]
    upper = lax.div(pair, pairs // 2)
    density = pltpu.roll(slots[0], upper * half, 1) + pltpu.roll(slots[1], (1 - upper) * half, 1)
    top = jnp.where((lane >= half) | (row < lane), packed, 0.0)
    bottom = pltpu.roll(jnp.where((lane < half) & (row > lane), packed, 0.0), half, 1)
    one_side = jnp.concatenate([top, bottom], axis=0)
    dist = one_side + one_side.T
    weight = (jnp.exp(-dist / feature_count) * density).astype(jnp.bfloat16)
    for step, ref in zip(steps + [(0, 0)], message_refs + [own_ref]):
        both = ref[half:].astype(jnp.float32)
        base = (pair ^ jnp.where(core == 0, step[0], step[1])) * CORES * rows
        for place in range(CORES):
            block = both[:, place * width : (place + 1) * width]
            vectors_ref[pl.ds(pl.multiple_of(base + place * rows, rows), rows), :] = block
    vectors = vectors_ref[...]
    own_rows = pl.ds(pl.multiple_of(me * rows, rows), rows)
    extended = jnp.concatenate(
        [vectors, jnp.ones((total, 1), jnp.float32), jnp.zeros((total, width - 1), jnp.float32)], axis=1
    )
    overlaps = lax.dot_general(
        vectors_ref[own_rows, :].astype(jnp.bfloat16),
        vectors.astype(jnp.bfloat16),
        (((1,), (1,)), ((), ())),
        preferred_element_type=jnp.float32,
    )
    left = jnp.concatenate([vectors.T, *pieces(overlaps)], axis=0).astype(jnp.bfloat16)
    numer = jnp.dot(weight, extended.astype(jnp.bfloat16), preferred_element_type=jnp.float32)
    applied = numer[:, :width] / numer[:, width : width + 1]
    applied_ref[...] = applied
    product = sum(
        jnp.dot(left, piece.astype(jnp.bfloat16), preferred_element_type=jnp.float32)
        for piece in reversed(pieces(applied))
    )
    coef_ref[...] = product[:width]
    projection = sum(product[width + part * rows :][:rows] for part in reversed(range(3)))
    residual_ref[...] = (applied_ref[own_rows, :] - projection / total).astype(jnp.bfloat16)


def from_peer(value, count, offsets):
    links = [(i, i ^ offsets[i % CORES]) for i in range(count) if offsets[i % CORES]]
    return lax.ppermute(value, "blk", links)


def shards(frames, basis, density):
    count = lax.axis_size("blk")
    rows, feature_count = frames.shape
    width = basis.shape[1]
    total = rows * count
    whole = pl.BlockSpec(memory_space=pltpu.VMEM)
    params = pltpu.CompilerParams(vmem_limit_bytes=48 << 20)
    features = lax.all_to_all(frames, "blk", split_axis=1, concat_axis=0, tiled=True)
    partial = pl.pallas_call(
        partial_kernel,
        out_shape=jax.ShapeDtypeStruct((total // 2 + rows, total), jnp.float32),
        in_specs=[whole] + [pl.BlockSpec(memory_space=pltpu.HBM)] * 2,
        out_specs=whole,
        scratch_shapes=[
            pltpu.VMEM(basis.shape, basis.dtype),
            pltpu.VMEM(density.shape, density.dtype),
            pltpu.SemaphoreType.DMA((2,)),
        ],
        compiler_params=params,
    )(
        features,
        pltpu.with_memory_space_constraint(basis, pltpu.HBM),
        pltpu.with_memory_space_constraint(density, pltpu.HBM),
    )
    sibling = (1, 1)
    message = (partial + from_peer(partial, count, sibling)).astype(jnp.bfloat16)
    received = [
        from_peer(message, count, (CORES * first, CORES * second))
        for first, second in routes(count // CORES)
    ]
    messages = [message] + received + [from_peer(part, count, sibling) for part in received]
    return pl.pallas_call(
        functools.partial(finish_kernel, feature_count, width, rows),
        out_shape=(
            jax.ShapeDtypeStruct((rows, width), jnp.bfloat16),
            jax.ShapeDtypeStruct((width, width), jnp.float32),
        ),
        in_specs=[whole] * len(messages),
        out_specs=(whole, whole),
        scratch_shapes=[pltpu.VMEM((total, width), jnp.float32)] * 2,
        compiler_params=params,
    )(*messages)


def solution(mesh):
    placed = (P(("groups", "blk"), None), P(("groups", "blk"), None), P(("groups", "blk")))
    return jax.shard_map(
        shards,
        mesh=mesh,
        in_specs=placed,
        out_specs=(P(("groups", "blk"), None), P("groups", None)),
        check_vma=False,
    )
```

```python
import functools

import jax
import jax.numpy as jnp
from jax import lax
from jax.experimental import pallas as pl
from jax.experimental.pallas import tpu as pltpu
from jax.sharding import PartitionSpec as P

CORES = 2


def partial_kernel(features_ref, basis_hbm, density_hbm, message_ref, basis_ref, density_ref, sems):
    copies = [
        pltpu.make_async_copy(basis_hbm, basis_ref, sems.at[0]),
        pltpu.make_async_copy(density_hbm, density_ref, sems.at[1]),
    ]
    for copy in copies:
        copy.start()
    features = features_ref[...]
    total = features.shape[0]
    half = total // 2
    rows, width = basis_ref.shape
    inner = lax.dot_general(
        features, features, (((1,), (1,)), ((), ())), preferred_element_type=jnp.float32
    )
    row = lax.broadcasted_iota(jnp.int32, (total, total), 0)
    lane = lax.broadcasted_iota(jnp.int32, (total, total), 1)
    diagonal = jnp.where(row == lane, inner, 0.0)
    dist = (
        jnp.sum(diagonal, axis=1, keepdims=True)
        + jnp.sum(diagonal, axis=0, keepdims=True)
        - 2.0 * inner
    )
    top, bottom = dist[:half], pltpu.roll(dist[half:], half, 1)
    own_row, own_lane = row[:half], lane[:half]
    packed = jnp.where((own_lane < half) & (own_row >= own_lane), bottom, top)

    for copy in copies:
        copy.wait()
    me = lax.axis_index("blk")
    density = density_ref[...].astype(jnp.float32).reshape(1, rows)
    density = jnp.concatenate([density, jnp.zeros((1, total - rows), jnp.float32)], axis=1)
    density = pltpu.roll(density, lax.rem(me * rows, half), 1)
    message_ref[:half] = jnp.where(own_row == own_lane, density, packed)
    vectors = jnp.concatenate(
        [basis_ref[...].astype(jnp.float32), jnp.zeros((rows, total - width), jnp.float32)], axis=1
    )
    message_ref[half:] = pltpu.roll(vectors, lax.rem(me, CORES) * width, 1)


def routes(pairs):
    half, quarter = pairs // 2, pairs // 4
    near = [(offset, offset + 1) for offset in range(2, half, 2)]
    return [(1, 1)] + near + [(half + step, half + quarter + step) for step in range(quarter)]


def pieces(value):
    high = value.astype(jnp.bfloat16).astype(jnp.float32)
    middle = (value - high).astype(jnp.bfloat16).astype(jnp.float32)
    return high, middle, (value - high - middle).astype(jnp.bfloat16).astype(jnp.float32)


def finish_kernel(feature_count, width, rows, *refs):
    residual_ref, coef_ref, applied_ref, vectors_ref = refs[-4:]
    own_ref, *message_refs = refs[:-4]
    half = own_ref.shape[1] // 2
    total = 2 * half
    pairs = total // (CORES * rows)
    me = lax.axis_index("blk")
    core, pair = lax.rem(me, CORES), lax.div(me, CORES)
    steps = routes(pairs)
    steps = steps + [(two, one) for one, two in steps[1:]]
    near = own_ref[:half].astype(jnp.float32)
    far = jnp.zeros_like(near)
    for step, ref in zip(steps, message_refs):
        if max(step) < pairs // 2:
            near += ref[:half].astype(jnp.float32)
        else:
            far += ref[:half].astype(jnp.float32)
    packed = near + far
    row = lax.broadcasted_iota(jnp.int32, (half, total), 0)
    lane = lax.broadcasted_iota(jnp.int32, (half, total), 1)
    slots = [
        jnp.sum(jnp.where(row == lane, part, 0.0), axis=0, keepdims=True) for part in (near, far)
    ]
    upper = lax.div(pair, pairs // 2)
    density = pltpu.roll(slots[0], upper * half, 1) + pltpu.roll(slots[1], (1 - upper) * half, 1)
    top = jnp.where((lane >= half) | (row < lane), packed, 0.0)
    bottom = pltpu.roll(jnp.where((lane < half) & (row > lane), packed, 0.0), half, 1)
    one_side = jnp.concatenate([top, bottom], axis=0)
    dist = one_side + one_side.T
    weight = (jnp.exp(-dist / feature_count) * density).astype(jnp.bfloat16)
    for step, ref in zip(steps + [(0, 0)], message_refs + [own_ref]):
        both = ref[half:].astype(jnp.float32)
        base = (pair ^ jnp.where(core == 0, step[0], step[1])) * CORES * rows
        for place in range(CORES):
            block = both[:, place * width : (place + 1) * width]
            vectors_ref[pl.ds(pl.multiple_of(base + place * rows, rows), rows), :] = block
    vectors = vectors_ref[...]
    own_rows = pl.ds(pl.multiple_of(me * rows, rows), rows)
    extended = jnp.concatenate(
        [vectors, jnp.ones((total, 1), jnp.float32), jnp.zeros((total, width - 1), jnp.float32)], axis=1
    )
    overlaps = lax.dot_general(
        vectors_ref[own_rows, :].astype(jnp.bfloat16),
        vectors.astype(jnp.bfloat16),
        (((1,), (1,)), ((), ())),
        preferred_element_type=jnp.float32,
    )
    left = jnp.concatenate([vectors.T, *pieces(overlaps)], axis=0).astype(jnp.bfloat16)
    numer = jnp.dot(weight, extended.astype(jnp.bfloat16), preferred_element_type=jnp.float32)
    applied = numer[:, :width] / numer[:, width : width + 1]
    applied_ref[...] = applied
    product = sum(
        jnp.dot(left, piece.astype(jnp.bfloat16), preferred_element_type=jnp.float32)
        for piece in reversed(pieces(applied))
    )
    coef_ref[...] = product[:width]
    projection = sum(product[width + part * rows :][:rows] for part in reversed(range(3)))
    residual_ref[...] = (applied_ref[own_rows, :] - projection / total).astype(jnp.bfloat16)


def from_peer(value, count, offsets):
    return lax.ppermute(value, "blk", [(i, i ^ offsets[i % CORES]) for i in range(count)])


def shards(frames, basis, density):
    count = lax.axis_size("blk")
    rows, feature_count = frames.shape
    width = basis.shape[1]
    total = rows * count
    whole = pl.BlockSpec(memory_space=pltpu.VMEM)
    params = pltpu.CompilerParams(vmem_limit_bytes=48 << 20)
    features = lax.all_to_all(frames, "blk", split_axis=1, concat_axis=0, tiled=True)
    partial = pl.pallas_call(
        partial_kernel,
        out_shape=jax.ShapeDtypeStruct((total // 2 + rows, total), jnp.float32),
        in_specs=[whole] + [pl.BlockSpec(memory_space=pltpu.HBM)] * 2,
        out_specs=whole,
        scratch_shapes=[
            pltpu.VMEM(basis.shape, basis.dtype),
            pltpu.VMEM(density.shape, density.dtype),
            pltpu.SemaphoreType.DMA((2,)),
        ],
        compiler_params=params,
    )(
        features,
        pltpu.with_memory_space_constraint(basis, pltpu.HBM),
        pltpu.with_memory_space_constraint(density, pltpu.HBM),
    )
    sibling = (1, 1)
    message = (partial + from_peer(partial, count, sibling)).astype(jnp.bfloat16)
    received = [
        from_peer(message, count, (CORES * first, CORES * second))
        for first, second in routes(count // CORES)
    ]
    messages = [message] + received + [from_peer(part, count, sibling) for part in received[1:]]
    return pl.pallas_call(
        functools.partial(finish_kernel, feature_count, width, rows),
        out_shape=(
            jax.ShapeDtypeStruct((rows, width), jnp.bfloat16),
            jax.ShapeDtypeStruct((width, width), jnp.float32),
        ),
        in_specs=[whole] * len(messages),
        out_specs=(whole, whole),
        scratch_shapes=[pltpu.VMEM((total, width), jnp.float32)] * 2,
        compiler_params=params,
    )(*messages)


def solution(mesh):
    placed = (P(("groups", "blk"), None), P(("groups", "blk"), None), P(("groups", "blk")))
    return jax.shard_map(
        shards,
        mesh=mesh,
        in_specs=placed,
        out_specs=(P(("groups", "blk"), None), P("groups", None)),
        check_vma=False,
    )
```

```python
import functools

import jax
import jax.numpy as jnp
from jax import lax
from jax.experimental import pallas as pl
from jax.experimental.pallas import tpu as pltpu
from jax.sharding import PartitionSpec as P

CORES = 2


def partial_kernel(features_ref, basis_ref, density_hbm, message_ref, density_ref, sem):
    copy = pltpu.make_async_copy(density_hbm, density_ref, sem)
    copy.start()
    features = features_ref[...]
    total = features.shape[0]
    half = total // 2
    rows, width = basis_ref.shape
    inner = lax.dot_general(
        features, features, (((1,), (1,)), ((), ())), preferred_element_type=jnp.float32
    )
    row = lax.broadcasted_iota(jnp.int32, (total, total), 0)
    lane = lax.broadcasted_iota(jnp.int32, (total, total), 1)
    diagonal = jnp.where(row == lane, inner, 0.0)
    dist = (
        jnp.sum(diagonal, axis=1, keepdims=True)
        + jnp.sum(diagonal, axis=0, keepdims=True)
        - 2.0 * inner
    )
    top, bottom = dist[:half], pltpu.roll(dist[half:], half, 1)
    own_row, own_lane = row[:half], lane[:half]
    packed = jnp.where((own_lane < half) & (own_row >= own_lane), bottom, top)

    copy.wait()
    me = lax.axis_index("blk")
    density = density_ref[...].astype(jnp.float32).reshape(1, rows)
    density = jnp.concatenate([density, jnp.zeros((1, total - rows), jnp.float32)], axis=1)
    density = pltpu.roll(density, lax.rem(me * rows, half), 1)
    message_ref[:half] = jnp.where(own_row == own_lane, density, packed)
    vectors = jnp.concatenate(
        [basis_ref[...].astype(jnp.float32), jnp.zeros((rows, total - width), jnp.float32)], axis=1
    )
    message_ref[half:] = pltpu.roll(vectors, lax.rem(me, CORES) * width, 1)


def routes(pairs):
    half = pairs // 2
    near = [(1, 3)] + [(offset, offset + 1) for offset in range(4, half, 2)]
    far = [
        step
        for base in range(half, pairs, 4)
        for step in ((base, base + 3), (base + 2, base + 1))
    ]
    return [(2, 2)] + near + far


def pieces(value):
    high = value.astype(jnp.bfloat16).astype(jnp.float32)
    middle = (value - high).astype(jnp.bfloat16).astype(jnp.float32)
    return high, middle, (value - high - middle).astype(jnp.bfloat16).astype(jnp.float32)


def finish_kernel(feature_count, width, rows, *refs):
    residual_ref, coef_ref, applied_ref, vectors_ref = refs[-4:]
    own_ref, *message_refs = refs[:-4]
    half = own_ref.shape[1] // 2
    total = 2 * half
    pairs = total // (CORES * rows)
    me = lax.axis_index("blk")
    core, pair = lax.rem(me, CORES), lax.div(me, CORES)
    steps = routes(pairs)
    steps = steps + [(two, one) for one, two in steps[1:]]
    near = own_ref[:half].astype(jnp.float32)
    far = jnp.zeros_like(near)
    for step, ref in zip(steps, message_refs):
        if max(step) < pairs // 2:
            near += ref[:half].astype(jnp.float32)
        else:
            far += ref[:half].astype(jnp.float32)
    packed = near + far
    row = lax.broadcasted_iota(jnp.int32, (half, total), 0)
    lane = lax.broadcasted_iota(jnp.int32, (half, total), 1)
    slots = [
        jnp.sum(jnp.where(row == lane, part, 0.0), axis=0, keepdims=True) for part in (near, far)
    ]
    upper = lax.div(pair, pairs // 2)
    density = pltpu.roll(slots[0], upper * half, 1) + pltpu.roll(slots[1], (1 - upper) * half, 1)
    top = jnp.where((lane >= half) | (row < lane), packed, 0.0)
    bottom = pltpu.roll(jnp.where((lane < half) & (row > lane), packed, 0.0), half, 1)
    one_side = jnp.concatenate([top, bottom], axis=0)
    dist = one_side + one_side.T
    weight = (jnp.exp(-dist / feature_count) * density).astype(jnp.bfloat16)
    for step, ref in zip(steps + [(0, 0)], message_refs + [own_ref]):
        both = ref[half:].astype(jnp.float32)
        base = (pair ^ jnp.where(core == 0, step[0], step[1])) * CORES * rows
        for place in range(CORES):
            block = both[:, place * width : (place + 1) * width]
            vectors_ref[pl.ds(pl.multiple_of(base + place * rows, rows), rows), :] = block
    vectors = vectors_ref[...]
    own_rows = pl.ds(pl.multiple_of(me * rows, rows), rows)
    extended = jnp.concatenate(
        [vectors, jnp.ones((total, 1), jnp.float32), jnp.zeros((total, width - 1), jnp.float32)], axis=1
    )
    overlaps = lax.dot_general(
        vectors_ref[own_rows, :].astype(jnp.bfloat16),
        vectors.astype(jnp.bfloat16),
        (((1,), (1,)), ((), ())),
        preferred_element_type=jnp.float32,
    )
    left = jnp.concatenate([vectors.T, *pieces(overlaps)], axis=0).astype(jnp.bfloat16)
    numer = jnp.dot(weight, extended.astype(jnp.bfloat16), preferred_element_type=jnp.float32)
    applied = numer[:, :width] / numer[:, width : width + 1]
    applied_ref[...] = applied
    product = sum(
        jnp.dot(left, piece.astype(jnp.bfloat16), preferred_element_type=jnp.float32)
        for piece in reversed(pieces(applied))
    )
    coef_ref[...] = product[:width]
    projection = sum(product[width + part * rows :][:rows] for part in reversed(range(3)))
    residual_ref[...] = (applied_ref[own_rows, :] - projection / total).astype(jnp.bfloat16)


def from_peer(value, count, offsets):
    return lax.ppermute(value, "blk", [(i, i ^ offsets[i % CORES]) for i in range(count)])


def shards(frames, basis, density):
    count = lax.axis_size("blk")
    rows, feature_count = frames.shape
    width = basis.shape[1]
    total = rows * count
    whole = pl.BlockSpec(memory_space=pltpu.VMEM)
    params = pltpu.CompilerParams(vmem_limit_bytes=48 << 20)
    features = lax.all_to_all(frames, "blk", split_axis=1, concat_axis=0, tiled=True)
    partial = pl.pallas_call(
        partial_kernel,
        out_shape=jax.ShapeDtypeStruct((total // 2 + rows, total), jnp.float32),
        in_specs=[whole] * 2 + [pl.BlockSpec(memory_space=pltpu.HBM)],
        out_specs=whole,
        scratch_shapes=[
            pltpu.VMEM(density.shape, density.dtype),
            pltpu.SemaphoreType.DMA(()),
        ],
        compiler_params=params,
    )(
        features,
        basis,
        pltpu.with_memory_space_constraint(density, pltpu.HBM),
    )
    sibling = (1, 1)
    message = (partial + from_peer(partial, count, sibling)).astype(jnp.bfloat16)
    received = [
        from_peer(message, count, (CORES * first, CORES * second))
        for first, second in routes(count // CORES)
    ]
    messages = [message] + received + [from_peer(part, count, sibling) for part in received[1:]]
    return pl.pallas_call(
        functools.partial(finish_kernel, feature_count, width, rows),
        out_shape=(
            jax.ShapeDtypeStruct((rows, width), jnp.bfloat16),
            jax.ShapeDtypeStruct((width, width), jnp.float32),
        ),
        in_specs=[whole] * len(messages),
        out_specs=(whole, whole),
        scratch_shapes=[pltpu.VMEM((total, width), jnp.float32)] * 2,
        compiler_params=params,
    )(*messages)


def solution(mesh):
    placed = (P(("groups", "blk"), None), P(("groups", "blk"), None), P(("groups", "blk")))
    return jax.shard_map(
        shards,
        mesh=mesh,
        in_specs=placed,
        out_specs=(P(("groups", "blk"), None), P("groups", None)),
        check_vma=False,
    )
```

```python
import functools

import jax
import jax.numpy as jnp
from jax import lax
from jax.experimental import pallas as pl
from jax.experimental.pallas import tpu as pltpu
from jax.sharding import PartitionSpec as P

CORES = 2


def partial_kernel(features_ref, basis_ref, density_hbm, message_ref, density_ref, sem):
    copy = pltpu.make_async_copy(density_hbm, density_ref, sem)
    copy.start()
    features = features_ref[...]
    total = features.shape[0]
    half = total // 2
    rows, width = basis_ref.shape
    inner = lax.dot_general(
        features, features, (((1,), (1,)), ((), ())), preferred_element_type=jnp.float32
    )
    row = lax.broadcasted_iota(jnp.int32, (total, total), 0)
    lane = lax.broadcasted_iota(jnp.int32, (total, total), 1)
    diagonal = jnp.where(row == lane, inner, 0.0)
    dist = (
        jnp.sum(diagonal, axis=1, keepdims=True)
        + jnp.sum(diagonal, axis=0, keepdims=True)
        - 2.0 * inner
    )
    top, bottom = dist[:half], pltpu.roll(dist[half:], half, 1)
    own_row, own_lane = row[:half], lane[:half]
    packed = jnp.where((own_lane < half) & (own_row >= own_lane), bottom, top)

    copy.wait()
    me = lax.axis_index("blk")
    density = density_ref[...].astype(jnp.float32).reshape(1, rows)
    density = jnp.concatenate([density, jnp.zeros((1, total - rows), jnp.float32)], axis=1)
    density = pltpu.roll(density, lax.rem(me * rows, half), 1)
    message_ref[:half] = jnp.where(own_row == own_lane, density, packed)
    vectors = jnp.concatenate(
        [basis_ref[...].astype(jnp.float32), jnp.zeros((rows, total - width), jnp.float32)], axis=1
    )
    message_ref[half:] = pltpu.roll(vectors, lax.rem(me, CORES) * width, 1)


def routes(pairs):
    half = pairs // 2
    near = [(1, 3)] + [(offset, offset + 1) for offset in range(4, half, 2)]
    far = [
        step
        for base in range(half, pairs, 4)
        for step in ((base, base + 3), (base + 2, base + 1))
    ]
    return [(2, 2)] + near + far


def pieces(value):
    high = value.astype(jnp.bfloat16).astype(jnp.float32)
    middle = (value - high).astype(jnp.bfloat16).astype(jnp.float32)
    return high, middle, (value - high - middle).astype(jnp.bfloat16).astype(jnp.float32)


def finish_kernel(feature_count, width, rows, *refs):
    residual_ref, coef_ref, applied_ref, vectors_ref = refs[-4:]
    own_ref, *message_refs = refs[:-4]
    half = own_ref.shape[1] // 2
    total = 2 * half
    pairs = total // (CORES * rows)
    me = lax.axis_index("blk")
    core, pair = lax.rem(me, CORES), lax.div(me, CORES)
    steps = routes(pairs)
    steps = steps + [(two, one) for one, two in steps[1:]]
    for step, ref in zip(steps + [(0, 0)], message_refs + [own_ref]):
        both = ref[half:].astype(jnp.float32)
        base = (pair ^ jnp.where(core == 0, step[0], step[1])) * CORES * rows
        for place in range(CORES):
            block = both[:, place * width : (place + 1) * width]
            vectors_ref[pl.ds(pl.multiple_of(base + place * rows, rows), rows), :] = block
    vectors = vectors_ref[...]
    own_rows = pl.ds(pl.multiple_of(me * rows, rows), rows)
    extended = jnp.concatenate(
        [vectors, jnp.ones((total, 1), jnp.float32), jnp.zeros((total, width - 1), jnp.float32)], axis=1
    )
    overlaps = lax.dot_general(
        vectors_ref[own_rows, :].astype(jnp.bfloat16),
        vectors.astype(jnp.bfloat16),
        (((1,), (1,)), ((), ())),
        preferred_element_type=jnp.float32,
    )
    left = jnp.concatenate([vectors.T, *pieces(overlaps)], axis=0).astype(jnp.bfloat16)
    near = own_ref[:half].astype(jnp.float32)
    far = jnp.zeros_like(near)
    for step, ref in zip(steps, message_refs):
        if max(step) < pairs // 2:
            near += ref[:half].astype(jnp.float32)
        else:
            far += ref[:half].astype(jnp.float32)
    packed = near + far
    row = lax.broadcasted_iota(jnp.int32, (half, total), 0)
    lane = lax.broadcasted_iota(jnp.int32, (half, total), 1)
    slots = [
        jnp.sum(jnp.where(row == lane, part, 0.0), axis=0, keepdims=True) for part in (near, far)
    ]
    upper = lax.div(pair, pairs // 2)
    density = pltpu.roll(slots[0], upper * half, 1) + pltpu.roll(slots[1], (1 - upper) * half, 1)
    top = jnp.where((lane >= half) | (row < lane), packed, 0.0)
    bottom = pltpu.roll(jnp.where((lane < half) & (row > lane), packed, 0.0), half, 1)
    one_side = jnp.concatenate([top, bottom], axis=0)
    dist = one_side + one_side.T
    weight = (jnp.exp(-dist / feature_count) * density).astype(jnp.bfloat16)
    numer = jnp.dot(weight, extended.astype(jnp.bfloat16), preferred_element_type=jnp.float32)
    applied = numer[:, :width] / numer[:, width : width + 1]
    applied_ref[...] = applied
    product = sum(
        jnp.dot(left, piece.astype(jnp.bfloat16), preferred_element_type=jnp.float32)
        for piece in reversed(pieces(applied))
    )
    coef_ref[...] = product[:width]
    projection = sum(product[width + part * rows :][:rows] for part in reversed(range(3)))
    residual_ref[...] = (applied_ref[own_rows, :] - projection / total).astype(jnp.bfloat16)


def from_peer(value, count, offsets):
    return lax.ppermute(value, "blk", [(i, i ^ offsets[i % CORES]) for i in range(count)])


def shards(frames, basis, density):
    count = lax.axis_size("blk")
    rows, feature_count = frames.shape
    width = basis.shape[1]
    total = rows * count
    whole = pl.BlockSpec(memory_space=pltpu.VMEM)
    params = pltpu.CompilerParams(vmem_limit_bytes=48 << 20)
    features = lax.all_to_all(frames, "blk", split_axis=1, concat_axis=0, tiled=True)
    partial = pl.pallas_call(
        partial_kernel,
        out_shape=jax.ShapeDtypeStruct((total // 2 + rows, total), jnp.float32),
        in_specs=[whole] * 2 + [pl.BlockSpec(memory_space=pltpu.HBM)],
        out_specs=whole,
        scratch_shapes=[
            pltpu.VMEM(density.shape, density.dtype),
            pltpu.SemaphoreType.DMA(()),
        ],
        compiler_params=params,
    )(
        features,
        basis,
        pltpu.with_memory_space_constraint(density, pltpu.HBM),
    )
    sibling = (1, 1)
    message = (partial + from_peer(partial, count, sibling)).astype(jnp.bfloat16)
    received = [
        from_peer(message, count, (CORES * first, CORES * second))
        for first, second in routes(count // CORES)
    ]
    messages = [message] + received + [from_peer(part, count, sibling) for part in received[1:]]
    return pl.pallas_call(
        functools.partial(finish_kernel, feature_count, width, rows),
        out_shape=(
            jax.ShapeDtypeStruct((rows, width), jnp.bfloat16),
            jax.ShapeDtypeStruct((width, width), jnp.float32),
        ),
        in_specs=[whole] * len(messages),
        out_specs=(whole, whole),
        scratch_shapes=[pltpu.VMEM((total, width), jnp.float32)] * 2,
        compiler_params=params,
    )(*messages)


def solution(mesh):
    placed = (P(("groups", "blk"), None), P(("groups", "blk"), None), P(("groups", "blk")))
    return jax.shard_map(
        shards,
        mesh=mesh,
        in_specs=placed,
        out_specs=(P(("groups", "blk"), None), P("groups", None)),
        check_vma=False,
    )
```
